32 devices in a mesh: clip: 8 (over y, x, core), frame: 4 (over z).
Axes of the slice: x: 2, y: 2, z: 4, core: 2. Of those that a mesh axis runs over, the one named last changes fastest.
Arguments:
- big_tokens: bfloat16 [8, 16, 256, 1024], P('clip', 'frame'), may hold values from -6 to 6
- small_tokens: bfloat16 [8, 16, 64, 1024], P('clip', 'frame'), may hold values from -6 to 6
- big_actions: int32 [8, 16], P('clip', 'frame'), may hold values from 0 to 7
- small_actions: int32 [8, 16], P('clip', 'frame'), may hold values from 0 to 7
- action_table: bfloat16 [8, 1024], P(None, ('clip', 'frame')), may hold values from -3 to 3
- norm_gain: bfloat16 [3, 1024], P(None, ('clip', 'frame')), may hold values from 0.099609375 to 1.8984375
- norm_bias: bfloat16 [3, 1024], P(None, ('clip', 'frame')), may hold values from -3 to 3
- spatial_inputs: bfloat16 [1024, 3072], P('frame', 'clip'), may hold values from -0.1875 to 0.1875
- spatial_output: bfloat16 [1024, 1024], P('frame', 'clip'), may hold values from -2 to 2
- temporal_inputs: bfloat16 [1024, 3072], P('frame', 'clip'), may hold values from -0.1875 to 0.1875
- temporal_output: bfloat16 [1024, 1024], P('frame', 'clip'), may hold values from -0.5 to 0.5
- up_weight: bfloat16 [1024, 4096], P('frame', 'clip'), may hold values from -0.1875 to 0.1875
- down_weight: bfloat16 [4096, 1024], P('frame', 'clip'), may hold values from -0.09375 to 0.09375
- branch_bias: bfloat16 [3, 1024], P(None, ('clip', 'frame')), may hold values from -2 to 2
- hidden_bias: bfloat16 [4096], P(('clip', 'frame')), may hold values from -3 to 3
- big_cotangent: bfloat16 [8, 16, 256, 1024], P('clip', 'frame'), may hold values from -6 to 6
- small_cotangent: bfloat16 [8, 16, 64, 1024], P('clip', 'frame'), may hold values from -6 to 6
Outputs:
- big_output: bfloat16 [8, 16, 256, 1024], P('clip', 'frame')
- small_output: bfloat16 [8, 16, 64, 1024], P('clip', 'frame')
- big_gradient: float32 [8, 16, 256, 1024], P('clip', 'frame')
- small_gradient: float32 [8, 16, 64, 1024], P('clip', 'frame')
- table_gradient: float32 [8, 1024], P(None, ('clip', 'frame'))
- gain_gradient: float32 [3, 1024], P(None, ('clip', 'frame'))
- bias_gradient: float32 [3, 1024], P(None, ('clip', 'frame'))
- spatial_inputs_gradient: float32 [1024, 3072], P('frame', 'clip')
- spatial_output_gradient: float32 [1024, 1024], P('frame', 'clip')
- temporal_inputs_gradient: float32 [1024, 3072], P('frame', 'clip')
- temporal_output_gradient: float32 [1024, 1024], P('frame', 'clip')
- up_gradient: float32 [1024, 4096], P('frame', 'clip')
- down_gradient: float32 [4096, 1024], P('frame', 'clip')
- branch_bias_gradient: float32 [3, 1024], P(None, ('clip', 'frame'))
- hidden_bias_gradient: float32 [4096], P(('clip', 'frame'))
The draws below stay inside these ranges and needn't reach their ends.
All inputs are finite; a program needn't handle non-finite values.
Results may differ from the reference program's by a relative error of at most 0.019.
Values may be sent and summed in bfloat16 or wider, within the bound.
No kernel may reach another device: no remote copies, remote signals or barrier semaphores. Data moves between devices by JAX's collectives and lax.ppermute only.
A program may use at most 320 MiB of HBM per device.

```python
import jax
import jax.numpy as jnp
from jax import lax

D = 1024
FF = 4096
ACTIONS = 8
HEAD_DIM = 64
FRAMES = 16
BIG_POS = 256
SMALL_POS = 64
BIG_CLIPS = 8
SMALL_CLIPS = 8


def plant(values, own_key, smallest, largest):
    longest = values.shape.index(max(values.shape))
    spots = []
    for shift in (0, 1):
        where = [jax.random.randint(jax.random.fold_in(own_key, axis), (), 0, length) for axis, length in enumerate(values.shape)]
        where[longest] = (where[longest] + shift) % values.shape[longest]
        spots.append(tuple(where))
    return values.at[spots[0]].set(smallest).at[spots[1]].set(largest)


def with_spikes(values, own_key, source, target, blocks, factor):
    def block_of(axis_at):
        return (jnp.arange(values.shape[axis_at]) // (values.shape[axis_at] // blocks)).reshape((-1,) + (1,) * (values.ndim - 1 - axis_at))

    first = jax.random.permutation(own_key, blocks)[block_of(target)]
    far = (block_of(target) + blocks // 2) % blocks
    return jnp.where((block_of(source) == first) | (block_of(source) == far), factor * values, values)


def shard_levels(key, shape, split, low, largest):
    level, own = 1.0, jax.random.fold_in(key, 6)
    for position, shards_of in split:
        heights = jnp.exp(jax.random.uniform(jax.random.fold_in(own, position), (shards_of,), jnp.float32, low / len(split), largest / len(split)))
        level = level * jnp.repeat(heights, shape[position] // shards_of).reshape([-1 if axis == position else 1 for axis in range(len(shape))])
    return level


def normal_values(own_key, shape, scale, limit, cuts=(), held_as=jnp.bfloat16):
    values = scale * jax.random.normal(own_key, shape, jnp.float32)
    if cuts:
        values = values * shard_levels(own_key, shape, cuts, -0.22, 0.18)
    return jnp.clip(values, -limit, limit).astype(held_as)


def bell_draw_with(key, dims, scale, bound, cuts, heavy, kind=jnp.bfloat16):
    values = scale * jax.random.normal(key, dims, jnp.float32)
    if cuts:
        values = values * shard_levels(key, dims, cuts, -0.22, 0.18)
    return jnp.clip(with_spikes(values, jax.random.fold_in(key, 3), *heavy), -bound, bound).astype(kind)


def setup_inputs(seed: int = 0) -> dict:
    seeds = jax.random.split(jax.random.key(seed), 18)
    return {
        "big_tokens": normal_values(seeds[0], (BIG_CLIPS, FRAMES, BIG_POS, D), 1.0, 6.0, ((0, 8), (1, 4))),
        "small_tokens": normal_values(seeds[1], (SMALL_CLIPS, FRAMES, SMALL_POS, D), 1.0, 6.0, ((0, 8), (1, 4))),
        "big_actions": plant(jax.random.randint(seeds[2], (BIG_CLIPS, FRAMES), 0, ACTIONS), jax.random.fold_in(seeds[2], 1), 0, ACTIONS - 1).astype(jnp.int32),
        "small_actions": plant(jax.random.randint(seeds[3], (SMALL_CLIPS, FRAMES), 0, ACTIONS), jax.random.fold_in(seeds[3], 1), 0, ACTIONS - 1).astype(jnp.int32),
        "action_table": normal_values(seeds[4], (ACTIONS, D), 0.5, 3.0, ((1, 32),)),
        "norm_gain": jnp.clip(1.0 + 0.18 * jax.random.normal(seeds[5], (3, D), jnp.float32), 0.099609375, 1.8984375).astype(jnp.bfloat16),
        "norm_bias": normal_values(seeds[6], (3, D), 0.5, 3.0, ((1, 32),)),
        "spatial_inputs": normal_values(seeds[7], (D, 3 * D), D ** -0.5, 0.1875, ((0, 4), (1, 8))),
        "spatial_output": normal_values(seeds[8], (D, D), (D // 128) ** -0.5, 2.0, ((0, 4), (1, 8))),
        "temporal_inputs": normal_values(seeds[9], (D, 3 * D), D ** -0.5, 0.1875, ((0, 4), (1, 8))),
        "temporal_output": normal_values(seeds[10], (D, D), (D // 8) ** -0.5, 0.5, ((0, 4), (1, 8))),
        "up_weight": normal_values(seeds[11], (D, FF), D ** -0.5, 0.1875, ((0, 4), (1, 8))),
        "down_weight": normal_values(seeds[12], (FF, D), FF ** -0.5, 0.09375, ((0, 4), (1, 8))),
        "branch_bias": normal_values(seeds[13], (3, D), 0.3, 2.0, ((1, 32),)),
        "hidden_bias": normal_values(seeds[14], (FF,), 0.5, 3.0, ((0, 32),)),
        "big_cotangent": bell_draw_with(seeds[15], (BIG_CLIPS, FRAMES, BIG_POS, D), 1.0, 6.0, ((0, 8), (1, 4)), (0, 3, 8, 2.0)),
        "small_cotangent": bell_draw_with(seeds[16], (SMALL_CLIPS, FRAMES, SMALL_POS, D), 1.0, 6.0, ((0, 8), (1, 4)), (1, 3, 4, 2.0)),
    }


@jax.custom_vjp
def low(v):
    return lax.optimization_barrier(v.astype(jnp.bfloat16)).astype(jnp.float32)

@jax.custom_vjp
def low_back(v):
    return v

def low_keep(v):
    return (low(v), None)

def low_pass(kept, grad):
    return (grad,)

def back_keep(v):
    return (v, None)

def back_low(kept, grad):
    return (low(grad),)
low.defvjp(low_keep, low_pass)
low_back.defvjp(back_keep, back_low)
EPSILON = 1e-05
SCORE_SCALE = 0.125
MASK_FILL = -1e+30
HIGHEST = lax.Precision.HIGHEST

def matmul(left_side, right_side):
    return jnp.dot(left_side, right_side, precision=HIGHEST, preferred_element_type=jnp.float32)

def layer_norm(values, norm_gain, offset):
    center = values - lax.optimization_barrier(jnp.mean(values, axis=-1, keepdims=True))
    spread = lax.optimization_barrier(jnp.mean(center * center, axis=-1, keepdims=True))
    return center * lax.rsqrt(spread + EPSILON) * norm_gain + offset

def attention(normed, weight_inputs, weight_out, bias_out, causal):
    head_count = weight_inputs.shape[1] // (3 * HEAD_DIM)
    packed = low_back(low(matmul(normed, weight_inputs)))
    pieces = packed.reshape(packed.shape[:-1] + (3, head_count, HEAD_DIM))
    query_rows = pieces[..., 0, :, :]
    key_rows = pieces[..., 1, :, :]
    value_rows = pieces[..., 2, :, :]
    scores = jnp.einsum('bqhd,bkhd->bhqk', query_rows, key_rows, precision=HIGHEST, preferred_element_type=jnp.float32) * SCORE_SCALE
    scores = low_back(scores)
    if causal:
        length = scores.shape[-1]
        allowed = jnp.arange(length, dtype=jnp.int32)[:, None] >= jnp.arange(length, dtype=jnp.int32)[None, :]
        scores = jnp.where(allowed, scores, MASK_FILL)
    weights = low(jax.nn.softmax(scores, axis=-1))
    mixture = jnp.einsum('bhqk,bkhd->bqhd', weights, value_rows, precision=HIGHEST, preferred_element_type=jnp.float32)
    mixture = low_back(low(mixture.reshape(mixture.shape[:2] + (-1,))))
    return low_back(matmul(mixture, weight_out) + bias_out)

def clip_forward(clip_tokens, action_ids, table, gains, biases, spatial_inputs, spatial_output, temporal_inputs, temporal_output, up_weight, down_weight, branch_bias, hidden_bias):
    onehot_rows = (action_ids[:, None] == jnp.arange(table.shape[0], dtype=jnp.int32)[None, :]).astype(jnp.float32)
    start = clip_tokens + matmul(onehot_rows, table)[:, None, :]
    spatial = start + attention(low(layer_norm(start, gains[0], biases[0])), spatial_inputs, spatial_output, branch_bias[0], False)
    spatial = low_back(low(spatial))
    across = jnp.swapaxes(spatial, 0, 1)
    temporal = across + attention(low(layer_norm(across, gains[1], biases[1])), temporal_inputs, temporal_output, branch_bias[1], True)
    temporal = jnp.swapaxes(low_back(low(temporal)), 0, 1)
    normed = low(layer_norm(temporal, gains[2], biases[2]))
    hidden = low_back(matmul(normed, up_weight) + hidden_bias)
    active = low(jax.nn.gelu(hidden, approximate=True))
    return temporal + low_back(matmul(active, down_weight) + branch_bias[2])

def run_batch(tokens, actions, cotangent, weight_set):

    def clip_step(running, clip_item):
        clip_tokens, clip_ids, clip_cotangent = clip_item

        def forward(start_tokens, *weight_list):
            return clip_forward(start_tokens, clip_ids, *weight_list)
        result, pullback = jax.vjp(forward, clip_tokens.astype(jnp.float32), *weight_set)
        gradients = pullback(clip_cotangent.astype(jnp.float32))
        running = tuple((earlier + update for earlier, update in zip(running, gradients[1:])))
        return (running, (result.astype(jnp.bfloat16), gradients[0]))
    initial = tuple((jnp.zeros(weight_array.shape, jnp.float32) for weight_array in weight_set))
    return lax.scan(clip_step, initial, (tokens, actions, cotangent))

def reference(big_tokens, small_tokens, big_actions, small_actions, action_table, norm_gain, norm_bias, spatial_inputs, spatial_output, temporal_inputs, temporal_output, up_weight, down_weight, branch_bias, hidden_bias, big_cotangent, small_cotangent):
    weight_set = tuple((array.astype(jnp.float32) for array in (action_table, norm_gain, norm_bias, spatial_inputs, spatial_output, temporal_inputs, temporal_output, up_weight, down_weight, branch_bias, hidden_bias)))
    big_sums, (big_output, big_gradient) = run_batch(big_tokens, big_actions, big_cotangent, weight_set)
    small_sums, (small_output, small_gradient) = run_batch(small_tokens, small_actions, small_cotangent, weight_set)
    totals = [from_big + from_small for from_big, from_small in zip(big_sums, small_sums)]
    return (big_output, small_output, big_gradient, small_gradient, totals[0], totals[1], totals[2], totals[3], totals[4], totals[5], totals[6], totals[7], totals[8], totals[9], totals[10])
```

```python
from functools import partial

import jax
import jax.numpy as jnp
from jax import lax
from jax.experimental import pallas as pl
from jax.experimental.pallas import tpu as pltpu
from jax.sharding import PartitionSpec as P

F32 = jnp.float32
BF16 = jnp.bfloat16
D = 1024
ROWS = 256
NEG = -1e30
EPS = 1e-05
VMEM_BYTES = 60 * 1024 * 1024


def nn(left, right):
    return lax.dot_general(left, right, (((1,), (0,)), ((), ())), preferred_element_type=F32)


def nt(left, right):
    return lax.dot_general(left, right, (((1,), (1,)), ((), ())), preferred_element_type=F32)


def tn(left, right):
    return lax.dot_general(left, right, (((0,), (0,)), ((), ())), preferred_element_type=F32)


def normal_parts(values):
    center = values - jnp.mean(values, axis=-1, keepdims=True)
    scale = lax.rsqrt(jnp.mean(center * center, axis=-1, keepdims=True) + EPS)
    return center * scale, scale


def normal_back(grad, normed, scale, gain):
    scaled = grad * gain
    first = jnp.mean(scaled, axis=-1, keepdims=True)
    second = jnp.mean(scaled * normed, axis=-1, keepdims=True)
    return scale * (scaled - first - normed * second)


def weight_copies(source, target, sems, width, base=0):
    blocks = source.shape[0]
    return [
        pltpu.make_async_copy(
            source.at[c], target.at[:, c * width : (c + 1) * width], sems.at[base + c]
        )
        for c in range(blocks)
    ]


def score_bias(spatial, step):
    rows = lax.broadcasted_iota(jnp.int32, (ROWS, ROWS), 0)
    cols = lax.broadcasted_iota(jnp.int32, (ROWS, ROWS), 1)
    if spatial:
        apart = jnp.logical_and((rows // 64) != (cols // 64), step == 4)
        return jnp.where(apart, NEG, 0.0)
    seen = jnp.logical_and(rows % 16 == cols % 16, rows // 16 >= cols // 16)
    return jnp.where(seen, 0.0, NEG)


def fwd_kernel(spatial, *refs):
    if spatial:
        x_ref, e_ref, small_ref, win_hbm, wo_hbm = refs[:5]
        refs = refs[5:]
    else:
        x_ref, small_ref, win_hbm, wo_hbm = refs[:4]
        refs = refs[4:]
    y_ref, qkv_ref, o_ref, lse_ref, win, wo, bias_s, sems = refs
    step = pl.program_id(0)
    copies_in = weight_copies(win_hbm, win, sems, 384)
    copies_out = weight_copies(wo_hbm, wo, sems, 128, 8)

    @pl.when(step == 0)
    def _():
        for copy in copies_in + copies_out:
            copy.start()

    if spatial:
        tokens = x_ref[0].astype(F32).reshape(4, 64, D)
        start = (tokens + e_ref[0][:, None, :]).reshape(ROWS, D)
        bias_s[...] = score_bias(True, step)
    else:
        start = x_ref[...].reshape(ROWS, D).astype(F32)

        @pl.when(step == 0)
        def _():
            bias_s[...] = score_bias(False, step)

    normed, _ = normal_parts(start)
    hidden = (normed * small_ref[0:1, :] + small_ref[1:2, :]).astype(BF16)

    @pl.when(step == 0)
    def _():
        for copy in copies_in + copies_out:
            copy.wait()

    for part in range(3):
        qkv_ref[0, :, part * D : (part + 1) * D] = nn(
            hidden, win[:, part * D : (part + 1) * D]
        ).astype(BF16)
    low = lax.broadcasted_iota(jnp.int32, (ROWS, 128), 1) < 64
    lane = lax.broadcasted_iota(jnp.int32, (ROWS, 128), 1)
    lse_all = jnp.zeros((ROWS, 128), F32)
    zero = jnp.zeros((ROWS, 128), BF16)
    for pair in range(8):
        at = pair * 128
        q2 = qkv_ref[0, :, at : at + 128] * jnp.asarray(0.125, BF16)
        k2 = qkv_ref[0, :, D + at : D + at + 128]
        v2 = qkv_ref[0, :, 2 * D + at : 2 * D + at + 128]
        mixed = []
        for half in range(2):
            qh = jnp.where(low, q2, zero) if half == 0 else jnp.where(low, zero, q2)
            scores = nt(qh, k2) + bias_s[...]
            top = jnp.max(scores, axis=-1, keepdims=True)
            expo = jnp.exp(scores - top)
            total = jnp.sum(expo, axis=-1, keepdims=True)
            mixed.append(nn(expo.astype(BF16), v2) * (1.0 / total))
            lse_all = jnp.where(lane == 2 * pair + half, top + jnp.log(total), lse_all)
        o_ref[0, :, at : at + 128] = jnp.where(low, mixed[0], mixed[1]).astype(BF16)
    lse_ref[0] = lse_all
    result = (start + (nn(o_ref[0], wo[...]) + small_ref[2:3, :])).astype(BF16)
    if spatial:

        @pl.when(step < 4)
        def _():
            y_ref[:, 0:4, step, :, :] = result.reshape(4, 4, 16, D)

        @pl.when(step == 4)
        def _():
            parts = result.reshape(4, 4, 16, D)
            for j in range(4):
                y_ref[j, 4, :, :, :] = parts[:, j]
    else:
        y_ref[...] = result.reshape(4, 1, 64, D)


def attention_forward(spatial, x, embed, small, win, wo):
    whole = pl.BlockSpec(memory_space=pl.ANY)
    small_spec = pl.BlockSpec((8, D), lambda s: (0, 0))
    if spatial:
        in_specs = [
            pl.BlockSpec((1, ROWS, D), lambda s: (s, 0, 0)),
            pl.BlockSpec((1, 4, D), lambda s: (s, 0, 0)),
            small_spec,
            whole,
            whole,
        ]
        operands = (x, embed, small, win, wo)
        y_spec = pl.BlockSpec((4, 5, 4, 16, D), lambda s: (0, 0, 0, 0, 0))
        y_shape = (4, 5, 4, 16, D)
    else:
        in_specs = [
            pl.BlockSpec((4, 1, 64, D), lambda s: (0, s, 0, 0)),
            small_spec,
            whole,
            whole,
        ]
        operands = (x, small, win, wo)
        y_spec = pl.BlockSpec((4, 1, 64, D), lambda s: (0, s, 0, 0))
        y_shape = (4, 5, 64, D)
    return pl.pallas_call(
        partial(fwd_kernel, spatial),
        grid=(5,),
        in_specs=in_specs,
        out_specs=[
            y_spec,
            pl.BlockSpec((1, ROWS, 3 * D), lambda s: (s, 0, 0)),
            pl.BlockSpec((1, ROWS, D), lambda s: (s, 0, 0)),
            pl.BlockSpec((1, ROWS, 128), lambda s: (s, 0, 0)),
        ],
        out_shape=[
            jax.ShapeDtypeStruct(y_shape, BF16),
            jax.ShapeDtypeStruct((5, ROWS, 3 * D), BF16),
            jax.ShapeDtypeStruct((5, ROWS, D), BF16),
            jax.ShapeDtypeStruct((5, ROWS, 128), F32),
        ],
        scratch_shapes=[
            pltpu.VMEM((D, 3 * D), BF16),
            pltpu.VMEM((D, D), BF16),
            pltpu.VMEM((ROWS, ROWS), F32),
            pltpu.SemaphoreType.DMA((16,)),
        ],
        compiler_params=pltpu.CompilerParams(
            dimension_semantics=("arbitrary",), vmem_limit_bytes=VMEM_BYTES
        ),
        cost_estimate=pl.CostEstimate(
            flops=2 * 1280 * D * 4 * D, bytes_accessed=30 * 1024 * 1024, transcendentals=5242880
        ),
        name="spatial_fwd" if spatial else "temporal_fwd",
    )(*operands)


def bwd_kernel(spatial, *refs):
    if spatial:
        g_ref, x_ref, e_ref, small_ref, qkv_ref, lse_ref, win_hbm, wo_hbm = refs[:8]
        big_ref, small_out_ref, frame_ref, h_ref, dqkv_ref, dy_ref, sums_ref = refs[8:15]
        win, wo, bias_s, do_s, sems = refs[15:]
    else:
        g_ref, x_ref, small_ref, qkv_ref, lse_ref, win_hbm, wo_hbm = refs[:7]
        dx_ref, h_ref, dqkv_ref, sums_ref = refs[7:11]
        win, wo, bias_s, do_s, sems = refs[11:]
    step = pl.program_id(0)
    copies_in = weight_copies(win_hbm, win, sems, 384)
    copies_out = weight_copies(wo_hbm, wo, sems, 128, 8)

    @pl.when(step == 0)
    def _():
        for copy in copies_in + copies_out:
            copy.start()
        sums_ref[...] = jnp.zeros((8, D), F32)

    if spatial:
        bias_s[...] = score_bias(True, step)

        @pl.when(step < 4)
        def _():
            dy_ref[0] = g_ref[:, 0:4, step, :, :].reshape(ROWS, D)

        @pl.when(step == 4)
        def _():
            for j in range(4):
                for f in range(4):
                    dy_ref[0, f * 64 + j * 16 : f * 64 + (j + 1) * 16, :] = g_ref[j, 4, f, :, :]

        grad = dy_ref[0]
    else:
        grad = g_ref[...].reshape(ROWS, D)

        @pl.when(step == 0)
        def _():
            bias_s[...] = score_bias(False, step)

    @pl.when(step == 0)
    def _():
        for copy in copies_in + copies_out:
            copy.wait()

    do_s[...] = nt(grad, wo[...]).astype(BF16)
    low = lax.broadcasted_iota(jnp.int32, (ROWS, 128), 1) < 64
    zero = jnp.zeros((ROWS, 128), BF16)
    eighth = jnp.asarray(0.125, BF16)

    def halves(value):
        return jnp.where(low, value, zero), jnp.where(low, zero, value)

    for pair in range(8):
        at = pair * 128
        q2 = halves(qkv_ref[0, :, at : at + 128] * eighth)
        k2 = qkv_ref[0, :, D + at : D + at + 128]
        kh = halves(k2 * eighth)
        v2 = qkv_ref[0, :, 2 * D + at : 2 * D + at + 128]
        do2 = halves(do_s[:, at : at + 128])
        dq = dk = dv = None
        for half in range(2):
            index = 2 * pair + half
            probs = jnp.exp(nt(q2[half], k2) + bias_s[...] - lse_ref[0, :, index : index + 1])
            dprobs = nt(do2[half], v2)
            inner = jnp.sum(probs * dprobs, axis=-1, keepdims=True)
            dscores = (probs * (dprobs - inner)).astype(BF16)
            dv_h = tn(probs.astype(BF16), do2[half])
            dk_h = tn(dscores, q2[half])
            dq_h = nn(dscores, kh[half])
            dq = dq_h if dq is None else dq + dq_h
            dk = dk_h if dk is None else dk + dk_h
            dv = dv_h if dv is None else dv + dv_h
        dqkv_ref[0, :, at : at + 128] = dq.astype(BF16)
        dqkv_ref[0, :, D + at : D + at + 128] = dk.astype(BF16)
        dqkv_ref[0, :, 2 * D + at : 2 * D + at + 128] = dv.astype(BF16)
    dh = nt(dqkv_ref[0], win[...])
    if spatial:
        tokens = x_ref[0].astype(F32).reshape(4, 64, D)
        start = (tokens + e_ref[0][:, None, :]).reshape(ROWS, D)
    else:
        start = x_ref[...].reshape(ROWS, D).astype(F32)
    normed, scale = normal_parts(start)
    gain = small_ref[0:1, :]
    h_ref[0] = (normed * gain + small_ref[1:2, :]).astype(BF16)
    grad32 = grad.astype(F32)
    total = grad32 + normal_back(dh, normed, scale, gain)
    sums_ref[0:1, :] += jnp.sum(dh * normed, axis=0, keepdims=True)
    sums_ref[1:2, :] += jnp.sum(dh, axis=0, keepdims=True)
    sums_ref[2:3, :] += jnp.sum(grad32, axis=0, keepdims=True)
    if spatial:
        frame_ref[0] = jnp.sum(total.reshape(4, 64, D), axis=1)

        @pl.when(step < 4)
        def _():
            big_ref[0] = total

        @pl.when(step == 4)
        def _():
            small_out_ref[...] = total
    else:
        dx_ref[...] = total.astype(BF16).reshape(4, 1, 64, D)


def attention_backward(spatial, grad, x, embed, small, qkv, lse, win, wo):
    whole = pl.BlockSpec(memory_space=pl.ANY)
    small_spec = pl.BlockSpec((8, D), lambda s: (0, 0))
    row_spec = pl.BlockSpec((1, ROWS, D), lambda s: (s, 0, 0))
    wide_spec = pl.BlockSpec((1, ROWS, 3 * D), lambda s: (s, 0, 0))
    lse_spec = pl.BlockSpec((1, ROWS, 128), lambda s: (s, 0, 0))
    group_spec = pl.BlockSpec((4, 1, 64, D), lambda s: (0, s, 0, 0))
    sums_spec = pl.BlockSpec((8, D), lambda s: (0, 0))
    rows_shape = jax.ShapeDtypeStruct((5, ROWS, D), BF16)
    wide_shape = jax.ShapeDtypeStruct((5, ROWS, 3 * D), BF16)
    sums_shape = jax.ShapeDtypeStruct((8, D), F32)
    if spatial:
        in_specs = [
            pl.BlockSpec((4, 5, 4, 16, D), lambda s: (0, 0, 0, 0, 0)),
            row_spec,
            pl.BlockSpec((1, 4, D), lambda s: (s, 0, 0)),
            small_spec,
            wide_spec,
            lse_spec,
            whole,
            whole,
        ]
        operands = (grad, x, embed, small, qkv, lse, win, wo)
        out_specs = [
            pl.BlockSpec((1, ROWS, D), lambda s: (jnp.minimum(s, 3), 0, 0)),
            pl.BlockSpec((ROWS, D), lambda s: (0, 0)),
            pl.BlockSpec((1, 4, D), lambda s: (s, 0, 0)),
            row_spec,
            wide_spec,
            row_spec,
            sums_spec,
        ]
        out_shape = [
            jax.ShapeDtypeStruct((4, ROWS, D), F32),
            jax.ShapeDtypeStruct((ROWS, D), F32),
            jax.ShapeDtypeStruct((5, 4, D), F32),
            rows_shape,
            wide_shape,
            rows_shape,
            sums_shape,
        ]
    else:
        in_specs = [group_spec, group_spec, small_spec, wide_spec, lse_spec, whole, whole]
        operands = (grad, x, small, qkv, lse, win, wo)
        out_specs = [group_spec, row_spec, wide_spec, sums_spec]
        out_shape = [
            jax.ShapeDtypeStruct((4, 5, 64, D), BF16),
            rows_shape,
            wide_shape,
            sums_shape,
        ]
    return pl.pallas_call(
        partial(bwd_kernel, spatial),
        grid=(5,),
        in_specs=in_specs,
        out_specs=out_specs,
        out_shape=out_shape,
        scratch_shapes=[
            pltpu.VMEM((D, 3 * D), BF16),
            pltpu.VMEM((D, D), BF16),
            pltpu.VMEM((ROWS, ROWS), F32),
            pltpu.VMEM((ROWS, D), BF16),
            pltpu.SemaphoreType.DMA((16,)),
        ],
        compiler_params=pltpu.CompilerParams(
            dimension_semantics=("arbitrary",), vmem_limit_bytes=VMEM_BYTES
        ),
        cost_estimate=pl.CostEstimate(
            flops=2 * 1280 * D * 4 * D, bytes_accessed=40 * 1024 * 1024, transcendentals=5242880
        ),
        name="spatial_bwd" if spatial else "temporal_bwd",
    )(*operands)


GELU_A = 0.7978845608028654
GELU_B = 0.044715
FF_CHUNK = 512


def ffn_kernel(x_ref, g_ref, small_ref, hb_ref, up_hbm, down_hbm, out_ref, dx_ref, h_ref, act_ref, du_ref, sums_ref, hsum_ref, up, down, acc, dacc, sems):
    step = pl.program_id(0)
    copies = weight_copies(up_hbm, up, sems, 512) + weight_copies(down_hbm, down, sems, 128, 8)

    @pl.when(step == 0)
    def _():
        for copy in copies:
            copy.start()
        sums_ref[...] = jnp.zeros((8, D), F32)
        hsum_ref[...] = jnp.zeros((1, 4 * D), F32)

    start = x_ref[...].astype(F32)
    normed, scale = normal_parts(start)
    gain = small_ref[0:1, :]
    hidden = (normed * gain + small_ref[1:2, :]).astype(BF16)
    h_ref[...] = hidden
    grad = g_ref[...]

    @pl.when(step == 0)
    def _():
        for copy in copies:
            copy.wait()

    for chunk in range(4 * D // FF_CHUNK):
        cols = slice(chunk * FF_CHUNK, (chunk + 1) * FF_CHUNK)
        u = nn(hidden, up[:, cols]) + hb_ref[:, cols]
        dact = nt(grad, down[cols, :])
        square = u * u
        inner = GELU_A * (u + GELU_B * (square * u))
        tanh = jnp.tanh(inner)
        half = 0.5 * (1.0 + tanh)
        act = (u * half).astype(BF16)
        slope = half + (0.5 * u) * (1.0 - tanh * tanh) * (GELU_A + (3.0 * GELU_A * GELU_B) * square)
        du = (slope * dact).astype(BF16)
        act_ref[:, cols] = act
        du_ref[:, cols] = du
        hsum_ref[:, cols] += jnp.sum(du.astype(F32), axis=0, keepdims=True)
    out_ref[...] = (start + (nn(act_ref[...], down[...]) + small_ref[2:3, :])).astype(BF16)
    dh = nt(du_ref[...], up[...])
    grad32 = grad.astype(F32)
    dx_ref[...] = (grad32 + normal_back(dh, normed, scale, gain)).astype(BF16)
    sums_ref[0:1, :] += jnp.sum(dh * normed, axis=0, keepdims=True)
    sums_ref[1:2, :] += jnp.sum(dh, axis=0, keepdims=True)
    sums_ref[2:3, :] += jnp.sum(grad32, axis=0, keepdims=True)


def ffn(x, grad, small, hidden_bias, up, down):
    rows = x.shape[0]
    tile = pl.BlockSpec((ROWS, D), lambda s: (s, 0))
    wide = pl.BlockSpec((ROWS, 4 * D), lambda s: (s, 0))
    whole = pl.BlockSpec(memory_space=pl.ANY)
    flat = jax.ShapeDtypeStruct((rows, D), BF16)
    wide_shape = jax.ShapeDtypeStruct((rows, 4 * D), BF16)
    return pl.pallas_call(
        ffn_kernel,
        grid=(rows // ROWS,),
        in_specs=[
            tile,
            tile,
            pl.BlockSpec((8, D), lambda s: (0, 0)),
            pl.BlockSpec((1, 4 * D), lambda s: (0, 0)),
            whole,
            whole,
        ],
        out_specs=[
            tile,
            tile,
            tile,
            wide,
            wide,
            pl.BlockSpec((8, D), lambda s: (0, 0)),
            pl.BlockSpec((1, 4 * D), lambda s: (0, 0)),
        ],
        out_shape=[
            flat,
            flat,
            flat,
            wide_shape,
            wide_shape,
            jax.ShapeDtypeStruct((8, D), F32),
            jax.ShapeDtypeStruct((1, 4 * D), F32),
        ],
        scratch_shapes=[
            pltpu.VMEM((D, 4 * D), BF16),
            pltpu.VMEM((4 * D, D), BF16),
            pltpu.VMEM((8, 128), F32),
            pltpu.VMEM((8, 128), F32),
            pltpu.SemaphoreType.DMA((16,)),
        ],
        compiler_params=pltpu.CompilerParams(
            dimension_semantics=("arbitrary",), vmem_limit_bytes=VMEM_BYTES
        ),
        cost_estimate=pl.CostEstimate(
            flops=8 * rows * D * 4 * D, bytes_accessed=50 * 1024 * 1024, transcendentals=5242880
        ),
        name="ffn",
    )(x, grad, small, hidden_bias, up, down)


def outer_kernel(left_ref, right_ref, out_ref):
    product = tn(left_ref[...], right_ref[...])
    blocks, _, width = out_ref.shape
    for c in range(blocks):
        out_ref[c] = product[:, c * width : (c + 1) * width].astype(BF16)


def outer(left, right, blocks, tile, name):
    rows, height = left.shape
    width = right.shape[1]
    each = width // blocks
    return pl.pallas_call(
        outer_kernel,
        grid=(height // tile,),
        in_specs=[
            pl.BlockSpec((rows, tile), lambda s: (0, s)),
            pl.BlockSpec((rows, width), lambda s: (0, 0)),
        ],
        out_specs=pl.BlockSpec((blocks, tile, each), lambda s: (0, s, 0)),
        out_shape=jax.ShapeDtypeStruct((blocks, height, each), BF16),
        compiler_params=pltpu.CompilerParams(
            dimension_semantics=("arbitrary",), vmem_limit_bytes=VMEM_BYTES
        ),
        cost_estimate=pl.CostEstimate(
            flops=2 * rows * height * width,
            bytes_accessed=2 * (rows * height + rows * width + height * width),
            transcendentals=0,
        ),
        name=name,
    )(left, right)


HEAD_DIM = 64


EPSILON = 1e-05
SCORE_SCALE = 0.125
MASK_FILL = -1e30
HIGHEST = lax.Precision.HIGHEST


def layer_norm(values, norm_gain, offset):
    center = values - jnp.mean(values, axis=-1, keepdims=True)
    spread = jnp.mean(center * center, axis=-1, keepdims=True)
    return center * lax.rsqrt(spread + EPSILON) * norm_gain + offset


def project(activation, weight):
    return jnp.dot(activation, weight, preferred_element_type=jnp.float32)


def outer_sum(left_side, right_side):
    flat_left = left_side.reshape(-1, left_side.shape[-1])
    flat_right = right_side.reshape(-1, right_side.shape[-1])
    return lax.dot_general(
        flat_left, flat_right, (((0,), (0,)), ((), ())), preferred_element_type=jnp.float32
    )


def through(gradient, weight):
    return lax.dot_general(
        gradient,
        weight,
        (((gradient.ndim - 1,), (1,)), ((), ())),
        preferred_element_type=jnp.float32,
    )


def combine_sets(earlier, later):
    return tuple((one_part + other_part for one_part, other_part in zip(earlier, later)))


def masked(scores, causal):
    if causal:
        length = scores.shape[-1]
        rows_index = lax.broadcasted_iota(jnp.int32, (length, length), 0)
        cols_index = lax.broadcasted_iota(jnp.int32, (length, length), 1)
        return jnp.where(rows_index >= cols_index, scores, MASK_FILL)
    return scores


def to_sequences(tensor, causal):
    if causal:
        tensor = jnp.swapaxes(tensor, 1, 2)
    return tensor.reshape((-1,) + tensor.shape[2:])


def from_sequences(tensor, leading, causal):
    if causal:
        return jnp.swapaxes(tensor.reshape((leading[0], leading[2], leading[1], -1)), 1, 2)
    return tensor.reshape(leading + (-1,))


def split_heads(packed, causal):
    head_count = packed.shape[-1] // (3 * HEAD_DIM)
    pieces = packed.reshape(packed.shape[:-1] + (3, head_count, HEAD_DIM))
    return tuple((to_sequences(pieces[..., member, :, :], causal) for member in range(3)))


def score_rows(query_rows, key_rows, causal):
    raw_scores = jnp.einsum(
        "bqhd,bkhd->bhqk", query_rows, key_rows, preferred_element_type=jnp.float32
    )
    return masked(raw_scores * SCORE_SCALE, causal)


def attend(query_rows, key_rows, value_rows, causal):
    scores = score_rows(query_rows, key_rows, causal)
    row_top = jnp.max(scores, axis=-1, keepdims=True)
    exponent = jnp.exp(scores - row_top)
    row_total = jnp.sum(exponent, axis=-1, keepdims=True)
    weights = (exponent / row_total).astype(jnp.bfloat16)
    mixture = jnp.einsum("bhqk,bkhd->bqhd", weights, value_rows, preferred_element_type=jnp.float32)
    return (mixture, row_top, row_total)


def attend_back(query_rows, key_rows, value_rows, row_top, row_total, grad_heads, causal):
    scores = score_rows(query_rows, key_rows, causal)
    probs = jnp.exp(scores - row_top) / row_total
    rounded = probs.astype(jnp.bfloat16)
    grad_value = jnp.einsum(
        "bhqk,bqhd->bkhd", rounded, grad_heads, preferred_element_type=jnp.float32
    )
    grad_probs = jnp.einsum(
        "bqhd,bkhd->bhqk", grad_heads, value_rows, preferred_element_type=jnp.float32
    )
    inner = jnp.sum(probs * grad_probs, axis=-1, keepdims=True)
    grad_scores = (probs * (grad_probs - inner)).astype(jnp.bfloat16)
    grad_query = (
        jnp.einsum("bhqk,bkhd->bqhd", grad_scores, key_rows, preferred_element_type=jnp.float32)
        * SCORE_SCALE
    )
    grad_key = (
        jnp.einsum("bhqk,bqhd->bkhd", grad_scores, query_rows, preferred_element_type=jnp.float32)
        * SCORE_SCALE
    )
    return (grad_query, grad_key, grad_value)


def mix_forward(start, norm_gain, offset, weight_inputs, weight_out, bias_out, causal):
    normed = layer_norm(start, norm_gain, offset).astype(jnp.bfloat16)
    packed = project(normed, weight_inputs).astype(jnp.bfloat16)
    query_rows, key_rows, value_rows = split_heads(packed, causal)
    attended, row_top, row_total = attend(query_rows, key_rows, value_rows, causal)
    mixture = from_sequences(attended, start.shape[:3], causal).astype(jnp.bfloat16)
    result = start + (project(mixture, weight_out) + bias_out)
    return (result.astype(jnp.bfloat16), (normed, packed, row_top, row_total, mixture))


def mix_backward(incoming, start, stored, norm_gain, offset, weight_inputs, weight_out, causal):
    normed, packed, row_top, row_total, mixture = stored
    leading = start.shape[:3]
    grad_out_weight = outer_sum(mixture, incoming)
    grad_out_bias = jnp.sum(incoming.astype(jnp.float32), axis=(0, 1, 2))
    grad_mixture = through(incoming, weight_out).astype(jnp.bfloat16)
    head_count = grad_mixture.shape[-1] // HEAD_DIM
    grad_heads = to_sequences(grad_mixture.reshape(leading + (head_count, HEAD_DIM)), causal)
    query_rows, key_rows, value_rows = split_heads(packed, causal)
    grad_parts = attend_back(
        query_rows, key_rows, value_rows, row_top, row_total, grad_heads, causal
    )
    grad_packed = jnp.concatenate(
        [from_sequences(part_grad, leading, causal) for part_grad in grad_parts], axis=-1
    ).astype(jnp.bfloat16)
    grad_in_weight = outer_sum(normed, grad_packed)
    grad_normed = through(grad_packed, weight_inputs)
    norm_pull = jax.vjp(layer_norm, start, norm_gain, offset)[1]
    grad_start, grad_gain, grad_offset = norm_pull(grad_normed)
    return (
        incoming.astype(jnp.float32) + grad_start,
        (grad_gain, grad_offset, grad_in_weight, grad_out_weight, grad_out_bias),
    )


def ffn_forward(start, norm_gain, offset, weight_up, bias_up, weight_down, bias_down):
    normed = layer_norm(start, norm_gain, offset).astype(jnp.bfloat16)
    hidden = project(normed, weight_up) + bias_up
    active = jax.nn.gelu(hidden, approximate=True).astype(jnp.bfloat16)
    result = start + (project(active, weight_down) + bias_down)
    return (result.astype(jnp.bfloat16), (normed, hidden, active))


def ffn_backward(cotangent, start, stored, norm_gain, offset, weight_up, weight_down):
    normed, hidden, active = stored
    grad_down = outer_sum(active, cotangent)
    grad_bias_down = jnp.sum(cotangent.astype(jnp.float32), axis=(0, 1, 2))
    grad_active = through(cotangent, weight_down)
    gelu_pull = jax.vjp(partial(jax.nn.gelu, approximate=True), hidden)[1]
    grad_hidden = gelu_pull(grad_active)[0].astype(jnp.bfloat16)
    grad_up = outer_sum(normed, grad_hidden)
    grad_bias_up = jnp.sum(grad_hidden.astype(jnp.float32), axis=(0, 1, 2))
    grad_normed = through(grad_hidden, weight_up)
    norm_pull = jax.vjp(layer_norm, start, norm_gain, offset)[1]
    grad_start, grad_gain, grad_offset = norm_pull(grad_normed)
    total_grad = (cotangent.astype(jnp.float32) + grad_start).astype(jnp.bfloat16)
    return (total_grad, (grad_gain, grad_offset, grad_up, grad_down, grad_bias_up, grad_bias_down))


def body(
    big_tokens,
    small_tokens,
    big_actions,
    small_actions,
    action_table,
    norm_gain,
    norm_bias,
    spatial_inputs,
    spatial_output,
    temporal_inputs,
    temporal_output,
    up_weight,
    down_weight,
    branch_bias,
    hidden_bias,
    big_cotangent,
    small_cotangent,
):
    (
        row_table,
        row_gain,
        row_bias,
        row_si,
        row_so,
        row_ti,
        row_to,
        row_up,
        row_down,
        row_branch,
        row_hidden,
    ) = (
        lax.all_gather(action_table, "frame", axis=1, tiled=True),
        lax.all_gather(norm_gain, "frame", axis=1, tiled=True),
        lax.all_gather(norm_bias, "frame", axis=1, tiled=True),
        lax.all_gather(spatial_inputs, "frame", axis=0, tiled=True),
        lax.all_gather(spatial_output, "frame", axis=0, tiled=True),
        lax.all_gather(temporal_inputs, "frame", axis=0, tiled=True),
        lax.all_gather(temporal_output, "frame", axis=0, tiled=True),
        lax.all_gather(up_weight, "frame", axis=0, tiled=True),
        lax.all_gather(down_weight, "frame", axis=0, tiled=True),
        lax.all_gather(branch_bias, "frame", axis=1, tiled=True),
        lax.all_gather(hidden_bias, "frame", axis=0, tiled=True),
    )
    (
        whole_table,
        whole_gain,
        whole_bias,
        whole_spatial_inputs,
        whole_spatial_output,
        whole_temporal_inputs,
        whole_temporal_output,
        whole_up,
        whole_down,
        whole_branch,
        whole_hidden,
    ) = (
        lax.all_gather(row_table, "clip", axis=1, tiled=True),
        lax.all_gather(row_gain, "clip", axis=1, tiled=True),
        lax.all_gather(row_bias, "clip", axis=1, tiled=True),
        lax.all_gather(row_si, "clip", axis=1, tiled=True),
        lax.all_gather(row_so, "clip", axis=1, tiled=True),
        lax.all_gather(row_ti, "clip", axis=1, tiled=True),
        lax.all_gather(row_to, "clip", axis=1, tiled=True),
        lax.all_gather(row_up, "clip", axis=1, tiled=True),
        lax.all_gather(row_down, "clip", axis=1, tiled=True),
        lax.all_gather(row_branch, "clip", axis=1, tiled=True),
        lax.all_gather(row_hidden, "clip", axis=0, tiled=True),
    )
    table_values = whole_table.astype(jnp.float32)
    gain_values = whole_gain.astype(jnp.float32)
    bias_values = whole_bias.astype(jnp.float32)
    branch_values = whole_branch.astype(jnp.float32)
    sub_batches = ((big_tokens, big_actions), (small_tokens, small_actions))
    cotangents = (big_cotangent, small_cotangent)
    onehot_list = []
    start_list = []
    spatial_sent = []
    spatial_stored = []
    for tokens, action_ids in sub_batches:
        onehot_rows = (
            action_ids[..., None] == jnp.arange(table_values.shape[0], dtype=jnp.int32)
        ).astype(jnp.float32)
        embedded = jnp.dot(
            onehot_rows, table_values, precision=HIGHEST, preferred_element_type=jnp.float32
        )
        start = tokens.astype(jnp.float32) + embedded[:, :, None, :]
        sent_rows, stored = mix_forward(
            start,
            gain_values[0],
            bias_values[0],
            whole_spatial_inputs,
            whole_spatial_output,
            branch_values[0],
            False,
        )
        onehot_list.append(onehot_rows)
        start_list.append(start)
        spatial_sent.append(sent_rows)
        spatial_stored.append(stored)
    by_position = (
        lax.all_to_all(spatial_sent[0], "frame", split_axis=2, concat_axis=1, tiled=True),
        lax.all_to_all(spatial_sent[1], "frame", split_axis=2, concat_axis=1, tiled=True),
    )
    residual_list = []
    temporal_sent = []
    temporal_stored = []
    for arriving in by_position:
        residual = arriving.astype(jnp.float32)
        sent_rows, stored = mix_forward(
            residual,
            gain_values[1],
            bias_values[1],
            whole_temporal_inputs,
            whole_temporal_output,
            branch_values[1],
            True,
        )
        residual_list.append(residual)
        temporal_sent.append(sent_rows)
        temporal_stored.append(stored)
    by_frame = (
        lax.all_to_all(temporal_sent[0], "frame", split_axis=1, concat_axis=2, tiled=True),
        lax.all_to_all(temporal_sent[1], "frame", split_axis=1, concat_axis=2, tiled=True),
    )
    hidden_values = whole_hidden.astype(jnp.float32)
    outputs = []
    back_sent = []
    ffn_total = None
    for member in range(2):
        start = by_frame[member].astype(jnp.float32)
        result, stored = ffn_forward(
            start,
            gain_values[2],
            bias_values[2],
            whole_up,
            hidden_values,
            whole_down,
            branch_values[2],
        )
        outputs.append(result)
        grad_sent, gradients = ffn_backward(
            cotangents[member], start, stored, gain_values[2], bias_values[2], whole_up, whole_down
        )
        back_sent.append(grad_sent)
        ffn_total = gradients if ffn_total is None else combine_sets(ffn_total, gradients)
    ffn_gain, ffn_offset, grad_up, grad_down, grad_hidden_bias, grad_down_bias = ffn_total
    back_position = (
        lax.all_to_all(back_sent[0], "frame", split_axis=2, concat_axis=1, tiled=True),
        lax.all_to_all(back_sent[1], "frame", split_axis=2, concat_axis=1, tiled=True),
    )
    temporal_back = []
    temporal_total = None
    for member in range(2):
        grad_start, gradients = mix_backward(
            back_position[member],
            residual_list[member],
            temporal_stored[member],
            gain_values[1],
            bias_values[1],
            whole_temporal_inputs,
            whole_temporal_output,
            True,
        )
        temporal_back.append(grad_start.astype(jnp.bfloat16))
        temporal_total = (
            gradients if temporal_total is None else combine_sets(temporal_total, gradients)
        )
    back_frame = (
        lax.all_to_all(temporal_back[0], "frame", split_axis=1, concat_axis=2, tiled=True),
        lax.all_to_all(temporal_back[1], "frame", split_axis=1, concat_axis=2, tiled=True),
    )
    input_grads = []
    spatial_total = None
    table_total = None
    for member in range(2):
        grad_start, gradients = mix_backward(
            back_frame[member],
            start_list[member],
            spatial_stored[member],
            gain_values[0],
            bias_values[0],
            whole_spatial_inputs,
            whole_spatial_output,
            False,
        )
        input_grads.append(grad_start)
        spatial_total = (
            gradients if spatial_total is None else combine_sets(spatial_total, gradients)
        )
        frame_sums = jnp.sum(grad_start, axis=2)
        table_part = jnp.einsum(
            "cfa,cfd->ad",
            onehot_list[member],
            frame_sums,
            precision=HIGHEST,
            preferred_element_type=jnp.float32,
        )
        table_total = table_part if table_total is None else table_total + table_part
    gain_stack = jnp.stack([spatial_total[0], temporal_total[0], ffn_gain])
    bias_stack = jnp.stack([spatial_total[1], temporal_total[1], ffn_offset])
    branch_stack = jnp.stack([spatial_total[4], temporal_total[4], grad_down_bias])
    (
        column_table,
        column_gain,
        column_bias,
        column_si,
        column_so,
        column_ti,
        column_to,
        column_up,
        column_down,
        column_branch,
        column_hidden,
    ) = (
        lax.psum_scatter(
            table_total.astype(jnp.bfloat16), "clip", scatter_dimension=1, tiled=True
        ).astype(jnp.float32),
        lax.psum_scatter(
            gain_stack.astype(jnp.bfloat16), "clip", scatter_dimension=1, tiled=True
        ).astype(jnp.float32),
        lax.psum_scatter(
            bias_stack.astype(jnp.bfloat16), "clip", scatter_dimension=1, tiled=True
        ).astype(jnp.float32),
        lax.psum_scatter(
            spatial_total[2].astype(jnp.bfloat16), "clip", scatter_dimension=1, tiled=True
        ).astype(jnp.float32),
        lax.psum_scatter(
            spatial_total[3].astype(jnp.bfloat16), "clip", scatter_dimension=1, tiled=True
        ).astype(jnp.float32),
        lax.psum_scatter(
            temporal_total[2].astype(jnp.bfloat16), "clip", scatter_dimension=1, tiled=True
        ).astype(jnp.float32),
        lax.psum_scatter(
            temporal_total[3].astype(jnp.bfloat16), "clip", scatter_dimension=1, tiled=True
        ).astype(jnp.float32),
        lax.psum_scatter(
            grad_up.astype(jnp.bfloat16), "clip", scatter_dimension=1, tiled=True
        ).astype(jnp.float32),
        lax.psum_scatter(
            grad_down.astype(jnp.bfloat16), "clip", scatter_dimension=1, tiled=True
        ).astype(jnp.float32),
        lax.psum_scatter(
            branch_stack.astype(jnp.bfloat16), "clip", scatter_dimension=1, tiled=True
        ).astype(jnp.float32),
        lax.psum_scatter(
            grad_hidden_bias.astype(jnp.bfloat16), "clip", scatter_dimension=0, tiled=True
        ).astype(jnp.float32),
    )
    (
        table_gradient,
        gain_gradient,
        bias_gradient,
        spatial_inputs_gradient,
        spatial_output_gradient,
        temporal_inputs_gradient,
        temporal_output_gradient,
        up_gradient,
        down_gradient,
        branch_bias_gradient,
        hidden_bias_gradient,
    ) = (
        lax.psum_scatter(
            column_table.astype(jnp.bfloat16), "frame", scatter_dimension=1, tiled=True
        ).astype(jnp.float32),
        lax.psum_scatter(
            column_gain.astype(jnp.bfloat16), "frame", scatter_dimension=1, tiled=True
        ).astype(jnp.float32),
        lax.psum_scatter(
            column_bias.astype(jnp.bfloat16), "frame", scatter_dimension=1, tiled=True
        ).astype(jnp.float32),
        lax.psum_scatter(
            column_si.astype(jnp.bfloat16), "frame", scatter_dimension=0, tiled=True
        ).astype(jnp.float32),
        lax.psum_scatter(
            column_so.astype(jnp.bfloat16), "frame", scatter_dimension=0, tiled=True
        ).astype(jnp.float32),
        lax.psum_scatter(
            column_ti.astype(jnp.bfloat16), "frame", scatter_dimension=0, tiled=True
        ).astype(jnp.float32),
        lax.psum_scatter(
            column_to.astype(jnp.bfloat16), "frame", scatter_dimension=0, tiled=True
        ).astype(jnp.float32),
        lax.psum_scatter(
            column_up.astype(jnp.bfloat16), "frame", scatter_dimension=0, tiled=True
        ).astype(jnp.float32),
        lax.psum_scatter(
            column_down.astype(jnp.bfloat16), "frame", scatter_dimension=0, tiled=True
        ).astype(jnp.float32),
        lax.psum_scatter(
            column_branch.astype(jnp.bfloat16), "frame", scatter_dimension=1, tiled=True
        ).astype(jnp.float32),
        lax.psum_scatter(
            column_hidden.astype(jnp.bfloat16), "frame", scatter_dimension=0, tiled=True
        ).astype(jnp.float32),
    )
    return (
        outputs[0],
        outputs[1],
        input_grads[0],
        input_grads[1],
        table_gradient,
        gain_gradient,
        bias_gradient,
        spatial_inputs_gradient,
        spatial_output_gradient,
        temporal_inputs_gradient,
        temporal_output_gradient,
        up_gradient,
        down_gradient,
        branch_bias_gradient,
        hidden_bias_gradient,
    )

def gather_weight(weight):
    gathered = lax.all_gather(weight, ("clip", "frame"))
    return gathered.reshape(8, 4 * weight.shape[0], weight.shape[1])


def scatter_weight(blocks):
    by_clip = lax.psum_scatter(blocks, "clip", scatter_dimension=0, tiled=False)
    return lax.psum_scatter(by_clip, "frame", scatter_dimension=0, tiled=True).astype(F32)


def exchange(values):
    return lax.all_to_all(values, "frame", 0, 0, tiled=True)


def to_groups(big, small):
    big_part = big.reshape(4, 4, 4, 16, D).transpose(1, 2, 0, 3, 4)
    small_part = small.reshape(4, 4, 1, 16, D).transpose(1, 2, 0, 3, 4)
    return jnp.concatenate([big_part, small_part], axis=1)


def from_groups(groups):
    big = groups[:, :4].transpose(2, 0, 1, 3, 4).reshape(1, 4, 256, D)
    small = groups[:, 4].transpose(1, 0, 2, 3).reshape(1, 4, 64, D)
    return big, small


def fast_body(
    big_tokens,
    small_tokens,
    big_actions,
    small_actions,
    action_table,
    norm_gain,
    norm_bias,
    spatial_inputs,
    spatial_output,
    temporal_inputs,
    temporal_output,
    up_weight,
    down_weight,
    branch_bias,
    hidden_bias,
    big_cotangent,
    small_cotangent,
):
    packed = jnp.concatenate(
        [
            action_table.reshape(-1),
            norm_gain.reshape(-1),
            norm_bias.reshape(-1),
            branch_bias.reshape(-1),
            hidden_bias,
        ]
    )
    smalls = lax.all_gather(packed, ("clip", "frame")).astype(F32)
    rows17 = smalls[:, :544].reshape(32, 17, 32).transpose(1, 0, 2).reshape(17, D)
    hidden_row = smalls[:, 544:].reshape(1, 4 * D)
    table = rows17[0:8]
    pad = jnp.zeros((5, D), F32)

    def small_of(index):
        return jnp.concatenate(
            [
                rows17[8 + index][None],
                rows17[11 + index][None],
                rows17[14 + index][None],
                pad,
            ]
        )

    smalls0, smalls1, smalls2 = small_of(0), small_of(1), small_of(2)
    big_ids = jnp.repeat(big_actions.reshape(4, 1), 4, axis=1)
    frame_ids = jnp.concatenate([big_ids, small_actions.reshape(1, 4)])
    onehot = (frame_ids[..., None] == jnp.arange(8, dtype=jnp.int32)).astype(F32)
    embed = jnp.sum(onehot[..., None] * table, axis=2)
    tokens = jnp.concatenate(
        [big_tokens.reshape(4, ROWS, D), small_tokens.reshape(1, ROWS, D)]
    )
    win_s = gather_weight(spatial_inputs)
    wo_s = gather_weight(spatial_output)
    win_t = gather_weight(temporal_inputs)
    wo_t = gather_weight(temporal_output)
    up = gather_weight(up_weight)
    down = gather_weight(down_weight)
    grads_out = to_groups(big_cotangent, small_cotangent)

    x1, qkv_s, o_s, lse_s = attention_forward(True, tokens, embed, smalls0, win_s, wo_s)
    x1p = exchange(x1).reshape(4, 5, 64, D)
    dyp = exchange(grads_out).reshape(1280, D)
    x2, qkv_t, o_t, lse_t = attention_forward(False, x1p, None, smalls1, win_t, wo_t)
    x2f = x2.reshape(1280, D)
    out, dx2, h3, act, du, sums2, hidden_sum = ffn(x2f, dyp, smalls2, hidden_row, up, down)
    outputs = from_groups(exchange(out.reshape(4, 5, 4, 16, D)))
    g_down = scatter_weight(outer(act, dyp, 8, 1024, "down_grad"))
    g_up = scatter_weight(outer(h3, du, 8, 256, "up_grad"))
    dx2g = dx2.reshape(4, 5, 64, D)
    dx1, h2, dqkv_t, sums1 = attention_backward(
        False, dx2g, x1p, None, smalls1, qkv_t, lse_t, win_t, wo_t
    )
    dx1f = exchange(dx1.reshape(4, 5, 4, 16, D))
    dx2o = dx2g.transpose(1, 0, 2, 3).reshape(1280, D)
    g_to = scatter_weight(outer(o_t.reshape(1280, D), dx2o, 8, 256, "temporal_out_grad"))
    g_ti = scatter_weight(
        outer(h2.reshape(1280, D), dqkv_t.reshape(1280, 3 * D), 8, 256, "temporal_in_grad")
    )
    big_grad, small_grad, frame_sums, h1, dqkv_s, dy1, sums0 = attention_backward(
        True, dx1f, tokens, embed, smalls0, qkv_s, lse_s, win_s, wo_s
    )
    g_so = scatter_weight(
        outer(o_s.reshape(1280, D), dy1.reshape(1280, D), 8, 256, "spatial_out_grad")
    )
    g_si = scatter_weight(
        outer(h1.reshape(1280, D), dqkv_s.reshape(1280, 3 * D), 8, 256, "spatial_in_grad")
    )
    table_sum = jnp.sum(
        onehot.reshape(20, 8)[:, :, None] * frame_sums.reshape(20, 1, D), axis=0
    )
    stacked = jnp.concatenate(
        [
            table_sum,
            sums0[0:1],
            sums1[0:1],
            sums2[0:1],
            sums0[1:2],
            sums1[1:2],
            sums2[1:2],
            sums0[2:3],
            sums1[2:3],
            sums2[2:3],
        ]
    )
    small_grads = jnp.concatenate(
        [
            stacked.reshape(17, 32, 32).transpose(1, 0, 2).reshape(32, 544),
            hidden_sum.reshape(32, 128),
        ],
        axis=1,
    )
    mine = lax.psum_scatter(small_grads, ("clip", "frame"), scatter_dimension=0, tiled=False)
    shard17 = mine[:544].reshape(17, 32)
    return (
        outputs[0],
        outputs[1],
        big_grad.reshape(1, 4, 256, D),
        small_grad.reshape(1, 4, 64, D),
        shard17[0:8],
        shard17[8:11],
        shard17[11:14],
        g_si,
        g_so,
        g_ti,
        g_to,
        g_up,
        g_down,
        shard17[14:17],
        mine[544:],
    )


def solution(mesh):
    placed = (
        P("clip", "frame", None, None),
        P("clip", "frame", None, None),
        P("clip", "frame"),
        P("clip", "frame"),
        P(None, ("clip", "frame")),
        P(None, ("clip", "frame")),
        P(None, ("clip", "frame")),
        P("frame", "clip"),
        P("frame", "clip"),
        P("frame", "clip"),
        P("frame", "clip"),
        P("frame", "clip"),
        P("frame", "clip"),
        P(None, ("clip", "frame")),
        P(("clip", "frame")),
        P("clip", "frame", None, None),
        P("clip", "frame", None, None),
    )
    return jax.shard_map(
        fast_body if dict(mesh.shape) == {"clip": 8, "frame": 4} else body,
        mesh=mesh,
        in_specs=placed,
        out_specs=(
            P("clip", "frame", None, None),
            P("clip", "frame", None, None),
            P("clip", "frame", None, None),
            P("clip", "frame", None, None),
            P(None, ("clip", "frame")),
            P(None, ("clip", "frame")),
            P(None, ("clip", "frame")),
            P("frame", "clip"),
            P("frame", "clip"),
            P("frame", "clip"),
            P("frame", "clip"),
            P("frame", "clip"),
            P("frame", "clip"),
            P(None, ("clip", "frame")),
            P(("clip", "frame")),
        ),
        check_vma=False,
    )
```
